32 devices in a mesh: req: 32 (over z, y, x, core).
Axes of the slice: x: 2, y: 2, z: 4, core: 2. Of those that a mesh axis runs over, the one named last changes fastest.
Arguments:
- hidden_in: bfloat16 [16384, 2048], P('req'), may hold values from -6 to 6
- qkv: bfloat16 [16384, 6144], P('req'), may hold values from -400 to 400
- cache: bfloat16 [128, 128, 4096], P('req'), may hold values from -400 to 400
- lengths: int32 [128], P('req'), may hold values from 2 to 128, as said below
- prefill_flag: int32 [32], P('req'), may hold values 0 or 1
- cache_slot: int32 [128], P('req'), may hold values from 0 to 127, as said below
- slot_owner: int32 [128], P('req'), may hold values from 0 to 127, as said below
- out_weight: bfloat16 [2048, 2048], replicated, may hold values from -0.125 to 0.125
Outputs:
- layer_out: bfloat16 [16384, 2048], P('req')
The draws below stay inside these ranges and needn't reach their ends.
Inputs may be any that keep to these rules, and one draw needn't show every extreme that they name: Each slot stores exactly one request's cache; of each device's 4 requests, at least half have their cache in a slot of their own device, drawn which; slot_owner[cache_slot[r]] = r. `slot_owner`: the inverse of cache_slot. `lengths`: some slot holds exactly 128 valid positions.
All inputs are finite; a program needn't handle non-finite values. No bound on the sum of `prefill_flag` on one device may be relied on, other than what follows from the above.
Results may differ from the reference program's by a relative error of at most 0.0034.
Values may be sent and summed in bfloat16 or wider, within the bound.
A program may use at most 128 MiB of HBM per device.

```python
import math
import jax
import jax.numpy as jnp
from jax import lax

D = 2048
H = 16
HD = 128
TOK_DEV = 512
RD = 4
LMAX = 128
ROWS = 16384
SLOTS = 128
N_REQ = 32


def slot_tables(key):
    base = jax.random.fold_in(key, 101)
    shuffle = jax.random.permutation(jax.random.fold_in(base, 1), N_REQ).astype(jnp.int32)
    device_keys = jax.random.split(jax.random.fold_in(base, 2), N_REQ)
    inner = jax.vmap(lambda sub: jax.random.permutation(sub, RD))(device_keys).astype(jnp.int32)
    device_ids = jnp.arange(N_REQ, dtype=jnp.int32)[:, None]
    positions = jnp.arange(RD, dtype=jnp.int32)[None, :]
    holders = jnp.where(positions < RD // 2, device_ids, shuffle[:, None])
    slot_ids = (holders * RD + positions).reshape(-1)
    request_ids = (device_ids * RD + inner).reshape(-1)
    cache_slot = jnp.zeros((SLOTS,), jnp.int32).at[request_ids].set(slot_ids)
    slot_owner = jnp.zeros((SLOTS,), jnp.int32).at[slot_ids].set(request_ids)
    return (cache_slot, slot_owner)


def first_keys(key):
    return jnp.clip(jax.random.normal(jax.random.fold_in(key, 102), (SLOTS, D), jnp.float32), -6.0, 6.0)


def base_values(key, shape):
    return jnp.clip(jax.random.normal(key, shape, jnp.float32), -6.0, 6.0)


def draw_cache_slot(key, part):
    return slot_tables(key)[0]


def draw_slot_owner(key, part):
    return slot_tables(key)[1]


def draw_lengths(key, part):
    drawn = jax.random.randint(jax.random.fold_in(key, 401), (SLOTS,), 2, LMAX + 1).astype(jnp.int32)
    chosen = jax.random.randint(jax.random.fold_in(key, 402), (), 0, SLOTS)
    return drawn.at[chosen].set(LMAX)


def draw_cache(key, part):
    values = base_values(jax.random.fold_in(key, 201), (SLOTS, LMAX, 2 * D))
    leading = first_keys(key)
    values = values.at[:, 0, :D].set(leading)
    return values.astype(jnp.bfloat16)


def draw_qkv(key, part):
    values = base_values(jax.random.fold_in(key, 301), (ROWS, 3 * D))
    return values.astype(jnp.bfloat16)


def set_ends(values, stream_key, least, largest):
    shape = values.shape
    spot = [jax.random.randint(jax.random.fold_in(stream_key, axis), (), 0, shape[axis]) for axis in range(len(shape))]
    values = values.at[tuple(spot)].set(least)
    longest = shape.index(max(shape))
    spot[longest] = (spot[longest] + 1) % shape[longest]
    return values.at[tuple(spot)].set(largest)


def block_levels(stream_key, extent, cuts, least, high):
    gain = 1.0
    for axis_at, blocks in cuts:
        steps = jax.random.uniform(jax.random.fold_in(jax.random.fold_in(stream_key, 6), axis_at), (blocks,), jnp.float32, least / len(cuts), high / len(cuts))
        gain = gain * jnp.repeat(jnp.exp(steps), extent[axis_at] // blocks).reshape((-1,) + (1,) * (len(extent) - 1 - axis_at))
    return gain


def scatter_about(key, dims, deviation, reach, cuts=(), kind=jnp.bfloat16):
    array = deviation * jax.random.normal(key, dims, jnp.float32)
    if cuts:
        array = array * block_levels(key, dims, cuts, -0.22, 0.18)
    return jnp.clip(array, -reach, reach).astype(kind)


def setup_inputs(seed: int = 0) -> dict:
    splits = jax.random.split(jax.random.key(seed), 9)
    return {
        "hidden_in": scatter_about(splits[0], (ROWS, D), 1.0, 6.0, ((0, 32),)),
        "qkv": draw_qkv(jax.random.fold_in(splits[8], 71), 0),
        "cache": draw_cache(jax.random.fold_in(splits[8], 71), 0),
        "lengths": draw_lengths(jax.random.fold_in(splits[8], 71), 0),
        "prefill_flag": set_ends((jax.random.randint(splits[4], (N_REQ,), 0, 2) < 1).astype(jnp.int32), jax.random.fold_in(splits[4], 1), 0, 1),
        "cache_slot": draw_cache_slot(jax.random.fold_in(splits[8], 71), 0),
        "slot_owner": draw_slot_owner(jax.random.fold_in(splits[8], 71), 0),
        "out_weight": scatter_about(splits[7], (D, D), D ** -0.5, 0.125),
    }


def prefill_block(block):
    score_scale = 1.0 / math.sqrt(HD)
    queries = block[:, :D].reshape(TOK_DEV, H, HD).astype(jnp.float32)
    keys_new = block[:, D:2 * D].reshape(TOK_DEV, H, HD).astype(jnp.float32)
    values_new = block[:, 2 * D:].reshape(TOK_DEV, H, HD).astype(jnp.float32)
    scores = jnp.einsum('qhd,khd->hqk', queries, keys_new) * score_scale
    causal = jnp.arange(TOK_DEV)[:, None] >= jnp.arange(TOK_DEV)[None, :]
    scores = jnp.where(causal[None], scores, -jnp.inf)
    top_score = lax.optimization_barrier(jnp.max(scores, axis=-1, keepdims=True))
    expon = jnp.exp(scores - top_score)
    totals = lax.optimization_barrier(jnp.sum(expon, axis=-1))
    rounded = lax.optimization_barrier(expon.astype(jnp.bfloat16)).astype(jnp.float32)
    summed = jnp.einsum('hqk,khd->qhd', rounded, values_new)
    result = summed / jnp.transpose(totals)[:, :, None]
    return result.reshape(TOK_DEV, D).astype(jnp.bfloat16)

def slot_partial(pieces):
    queries, stored, slot_lengths = pieces
    score_scale = 1.0 / math.sqrt(HD)
    query_heads = queries.reshape(RD, H, HD).astype(jnp.float32)
    cache_keys = stored[:, :, :D].reshape(RD, LMAX, H, HD).astype(jnp.float32)
    cache_values = stored[:, :, D:].reshape(RD, LMAX, H, HD).astype(jnp.float32)
    valid = jnp.arange(LMAX, dtype=jnp.int32)[None, None, :] < slot_lengths[:, None, None]
    scores = jnp.einsum('rhd,rlhd->rhl', query_heads, cache_keys) * score_scale
    scores = jnp.where(valid, scores, -jnp.inf)
    cache_max = lax.optimization_barrier(jnp.max(scores, axis=-1))
    expon = jnp.exp(scores - cache_max[..., None])
    cache_total = lax.optimization_barrier(jnp.sum(expon, axis=-1))
    rounded = lax.optimization_barrier(expon.astype(jnp.bfloat16)).astype(jnp.float32)
    cache_out = jnp.einsum('rhl,rlhd->rhd', rounded, cache_values)
    return (cache_out, cache_max, cache_total)

def reference(hidden_in, qkv, cache, lengths, prefill_flag, cache_slot, slot_owner, out_weight):
    blocks = qkv.reshape(N_REQ, TOK_DEV, 3 * D)
    prefill_att = lax.map(prefill_block, blocks)
    request_rows = blocks[:, :RD, :].reshape(SLOTS, 3 * D)
    slot_queries = request_rows[slot_owner][:, :D]
    part_out, part_max, part_total = lax.map(slot_partial, (slot_queries.reshape(N_REQ, RD, D), cache.reshape(N_REQ, RD, LMAX, 2 * D), lengths.reshape(N_REQ, RD)))
    part_out = part_out.reshape(SLOTS, H, HD)[cache_slot]
    part_max = part_max.reshape(SLOTS, H)[cache_slot]
    part_total = part_total.reshape(SLOTS, H)[cache_slot]
    score_scale = 1.0 / math.sqrt(HD)
    queries = request_rows[:, :D].reshape(SLOTS, H, HD).astype(jnp.float32)
    keys_new = request_rows[:, D:2 * D].reshape(SLOTS, H, HD).astype(jnp.float32)
    values_new = request_rows[:, 2 * D:].reshape(SLOTS, H, HD).astype(jnp.float32)
    own_score = lax.optimization_barrier(jnp.sum(queries * keys_new, axis=-1)) * score_scale
    joint_max = jnp.maximum(part_max, own_score)
    cache_factor = jnp.exp(part_max - joint_max)
    own_factor = jnp.exp(own_score - joint_max)
    numer = part_out * cache_factor[..., None] + own_factor[..., None] * values_new
    denom = part_total * cache_factor + own_factor
    decode_att = (numer / denom[..., None]).reshape(N_REQ, RD, D).astype(jnp.bfloat16)
    padding = jnp.zeros((N_REQ, TOK_DEV - RD, D), jnp.bfloat16)
    decode_rows = jnp.concatenate([decode_att, padding], axis=1)
    attended = jnp.where(prefill_flag[:, None, None] == 1, prefill_att, decode_rows)
    projected = jnp.dot(attended.reshape(ROWS, D), out_weight, preferred_element_type=jnp.float32).astype(jnp.bfloat16)
    summed = hidden_in.astype(jnp.float32) + projected.astype(jnp.float32)
    return summed.astype(jnp.bfloat16)
```

```python
import functools
import math

import jax
import jax.numpy as jnp
from jax import lax
from jax.experimental import pallas as pl
from jax.experimental.pallas import tpu as pltpu
from jax.sharding import PartitionSpec as P

D = 2048
H = 16
HD = 128
TOK_DEV = 512
RD = 4
LMAX = 128
NB = 8
HALF = TOK_DEV // 2
SEG = 4
COLS = SEG * HD
NT = 256
SCALE = 1.0 / math.sqrt(HD)
SCALE2 = SCALE * math.log2(math.e)
F32 = jnp.float32
BF16 = jnp.bfloat16
MESH = pl.DeviceIdType.MESH
NEG = float(jnp.finfo(jnp.float32).min)


def attend_head(h, qkv, att):
    col = pl.multiple_of(h * HD, HD)
    ones = jnp.ones((TOK_DEV, HD), BF16)
    keys = qkv[1, :, pl.ds(col, HD)]
    values = jnp.concatenate([qkv[2, :, pl.ds(col, HD)], ones], axis=1)
    row = lax.broadcasted_iota(jnp.int32, (HALF, HALF), 0)
    lane = lax.broadcasted_iota(jnp.int32, (HALF, HALF), 1)
    causal = lane <= row
    for part in range(2):
        rows = pl.ds(part * HALF, HALF)
        q = qkv[0, rows, pl.ds(col, HD)]
        blocks = []
        for kb in range(part + 1):
            s = lax.dot_general(
                q,
                keys[kb * HALF : (kb + 1) * HALF],
                (((1,), (1,)), ((), ())),
                preferred_element_type=F32,
            )
            blocks.append(jnp.where(causal, s, NEG) if kb == part else s)
        top = jnp.max(blocks[0], axis=1, keepdims=True)
        for s in blocks[1:]:
            top = jnp.maximum(top, jnp.max(s, axis=1, keepdims=True))
        acc = None
        for kb, s in enumerate(blocks):
            p = jnp.exp2((s - top) * SCALE2).astype(BF16)
            o = jnp.dot(p, values[kb * HALF : (kb + 1) * HALF], preferred_element_type=F32)
            acc = o if acc is None else acc + o
        att[rows, pl.ds(col, HD)] = (acc[:, :HD] / acc[:, HD:]).astype(BF16)


def head_mask():
    row = lax.broadcasted_iota(jnp.int32, (H, D), 0)
    lane = lax.broadcasted_iota(jnp.int32, (H, D), 1)
    return (lane // HD) == row


def pick_row(block, j):
    row = lax.broadcasted_iota(jnp.int32, block.shape, 0)
    return jnp.sum(jnp.where(row == j, block.astype(F32), 0.0), axis=0, keepdims=True)


def pick_lane(block, j):
    lane = lax.broadcasted_iota(jnp.int32, block.shape, 1)
    return jnp.sum(jnp.where(lane == j, block, 0.0), axis=1, keepdims=True)


def kernel(
    na,
    lengths,
    flag,
    cache_slot,
    slot_owner,
    qkv_hbm,
    cache_hbm,
    weight_hbm,
    out_hbm,
    first,
    qkv,
    cache,
    weight,
    att,
    result,
    qg,
    cg,
    sg,
    in_sem,
    out_sem,
    sa,
    ra,
    sb,
    rb,
    sc,
    rc,
    sd,
    rd,
    se,
    re,
    sf,
    rf,
):
    me = lax.axis_index("req")
    a = me // NB
    b = me % NB

    def peer_a(t):
        return lax.rem(a + t, na) * NB + b

    def peer_b(t):
        return a * NB + lax.rem(b + t, NB)

    loads = [pltpu.make_async_copy(qkv_hbm.at[pl.ds(0, 16), :], first, in_sem.at[0])]
    for g in range(H // SEG):
        for part in range(3):
            loads.append(
                pltpu.make_async_copy(
                    qkv_hbm.at[:, pl.ds(part * D + g * COLS, COLS)],
                    qkv.at[part, :, pl.ds(g * COLS, COLS)],
                    in_sem.at[1 + g * 3 + part],
                )
            )
    load_cache = pltpu.make_async_copy(cache_hbm, cache, in_sem.at[13])
    load_weight = pltpu.make_async_copy(weight_hbm, weight, in_sem.at[14])
    for load in loads[:7]:
        load.start()
    load_cache.start()
    for load in loads[7:]:
        load.start()
    load_weight.start()

    barrier = pltpu.get_barrier_semaphore()

    @pl.loop(1, na)
    def _(t):
        pl.semaphore_signal(barrier, inc=1, device_id=(peer_a(t),), device_id_type=MESH)

    @pl.loop(1, NB)
    def _(t):
        pl.semaphore_signal(barrier, inc=1, device_id=(peer_b(t),), device_id_type=MESH)

    loads[0].wait()
    qg[b, a] = first[:, :D].astype(F32)[:RD].astype(BF16)
    pl.semaphore_wait(barrier, na - 1 + NB - 1)

    def copy_a(buf, send, recv, t):
        return pltpu.make_async_remote_copy(
            src_ref=buf.at[b, a],
            dst_ref=buf.at[b, a],
            send_sem=send.at[t - 1],
            recv_sem=recv.at[t - 1],
            device_id=(peer_a(t),),
            device_id_type=MESH,
        )

    def copy_b(buf, send, recv, t):
        return pltpu.make_async_remote_copy(
            src_ref=buf.at[b],
            dst_ref=buf.at[b],
            send_sem=send.at[t - 1],
            recv_sem=recv.at[t - 1],
            device_id=(peer_b(t),),
            device_id_type=MESH,
        )

    def start_a(buf, send, recv):
        @pl.loop(1, na)
        def _(t):
            copy_a(buf, send, recv, t).start()

    def wait_a(buf, send, recv):
        @pl.loop(1, na)
        def _(t):
            copy_a(buf, send, recv, t).wait()

    def start_b(buf, send, recv):
        @pl.loop(1, NB)
        def _(t):
            copy_b(buf, send, recv, t).start()

    def wait_b(buf, send, recv):
        @pl.loop(1, NB)
        def _(t):
            copy_b(buf, send, recv, t).wait()

    def segment(g):
        for load in loads[1 + 3 * g : 4 + 3 * g]:
            load.wait()

        @pl.loop(g * SEG, (g + 1) * SEG)
        def _(h):
            attend_head(h, qkv, att)

    start_a(qg, sa, ra)
    segment(0)
    wait_a(qg, sa, ra)
    start_b(qg, sb, rb)
    segment(1)
    load_cache.wait()
    wait_b(qg, sb, rb)

    own = head_mask()
    row4 = lax.broadcasted_iota(jnp.int32, (RD, D), 0)
    lane_h = lax.broadcasted_iota(jnp.int32, (H, LMAX), 1)
    sums = jnp.zeros((RD, D), F32)
    stats = jnp.zeros((H, 128), F32)
    for s in range(RD):
        owner = slot_owner[s]
        device = owner // RD
        block = qg[device % NB, device // NB]
        q = pick_row(block, owner % RD)
        q_heads = jnp.where(own, q, 0.0).astype(BF16)
        scores = lax.dot_general(
            q_heads, cache[s, :, :D], (((1,), (1,)), ((), ())), preferred_element_type=F32
        )
        scores = jnp.where(lane_h < lengths[s], scores, NEG)
        top = jnp.max(scores, axis=1, keepdims=True)
        p = jnp.where(lane_h < lengths[s], jnp.exp2((scores - top) * SCALE2), 0.0)
        total = jnp.sum(p, axis=1, keepdims=True)
        o = jnp.dot(p.astype(BF16), cache[s, :, D:], preferred_element_type=F32)
        o = jnp.sum(jnp.where(own, o / total, 0.0), axis=0, keepdims=True)
        sums = jnp.where(row4 == s, o, sums)
        stats = jnp.where(lane_h == s, top * SCALE, jnp.where(lane_h == RD + s, total, stats))
    cg[b, a] = sums.astype(BF16)
    sg[b, a] = stats

    start_a(cg, sc, rc)
    start_a(sg, sd, rd)
    segment(2)
    wait_a(cg, sc, rc)
    wait_a(sg, sd, rd)
    start_b(cg, se, re)
    start_b(sg, sf, rf)
    segment(3)
    load_weight.wait()
    is_prefill = flag[0] == 1

    def project(part):
        @pl.loop(0, D // NT)
        def _(n):
            cols = pl.ds(pl.multiple_of(n * NT, NT), NT)
            rows = pl.ds(part * HALF, HALF)
            acc = jnp.dot(att[rows, :], weight[:, cols], preferred_element_type=F32)
            if part == 1:
                acc = jnp.where(is_prefill, acc, 0.0)
            result[rows, cols] = acc.astype(BF16)

        return pltpu.make_async_copy(
            result.at[pl.ds(part * HALF, HALF), :],
            out_hbm.at[pl.ds(part * HALF, HALF), :],
            out_sem.at[part],
        )

    lower = project(1)
    lower.start()
    wait_b(cg, se, re)
    wait_b(sg, sf, rf)

    row16 = lax.broadcasted_iota(jnp.int32, (H, D), 0)
    decoded = jnp.zeros((H, D), F32)
    for j in range(RD):
        slot = cache_slot[j]
        device = slot // RD
        co = pick_row(cg[device % NB, device // NB], slot % RD)
        stat = sg[device % NB, device // NB]
        cm = pick_lane(stat, slot % RD)
        cl = pick_lane(stat, RD + slot % RD)
        mine = first[...].astype(F32)[j : j + 1]
        product = mine[:, :D] * mine[:, D : 2 * D]
        ns = jnp.sum(jnp.where(own, product, 0.0), axis=1, keepdims=True) * SCALE
        joint = jnp.maximum(cm, ns)
        wc = cl * jnp.exp(cm - joint)
        wo = jnp.exp(ns - joint)
        mixed = (co * wc + mine[:, 2 * D :] * wo) / (wc + wo)
        decoded = jnp.where(
            row16 == j, jnp.sum(jnp.where(own, mixed, 0.0), axis=0, keepdims=True), decoded
        )
    kept = jnp.where(is_prefill, att[pl.ds(0, H), :].astype(F32), decoded)
    att[pl.ds(0, H), :] = kept.astype(BF16)
    rest = att[pl.ds(H, HALF - H), :]
    att[pl.ds(H, HALF - H), :] = jnp.where(is_prefill, rest, jnp.zeros_like(rest))
    upper = project(0)
    upper.start()
    lower.wait()
    upper.wait()


def local(hidden_in, qkv, cache, lengths, prefill_flag, cache_slot, slot_owner, out_weight, n):
    na = n // NB
    smem = pl.BlockSpec(memory_space=pltpu.SMEM)
    hbm = pl.BlockSpec(memory_space=pl.ANY)
    dma = pltpu.SemaphoreType.DMA
    projected = pl.pallas_call(
        functools.partial(kernel, na),
        out_shape=jax.ShapeDtypeStruct((TOK_DEV, D), BF16),
        in_specs=[smem] * 4 + [hbm] * 3,
        out_specs=hbm,
        scratch_shapes=[
            pltpu.VMEM((16, 3 * D), BF16),
            pltpu.VMEM((3, TOK_DEV, D), BF16),
            pltpu.VMEM((RD, LMAX, 2 * D), BF16),
            pltpu.VMEM((D, D), BF16),
            pltpu.VMEM((TOK_DEV, D), BF16),
            pltpu.VMEM((TOK_DEV, D), BF16),
            pltpu.VMEM((NB, na, RD, D), BF16),
            pltpu.VMEM((NB, na, RD, D), BF16),
            pltpu.VMEM((NB, na, H, 128), F32),
            dma((15,)),
            dma((2,)),
            dma((na - 1,)),
            dma((na - 1,)),
            dma((NB - 1,)),
            dma((NB - 1,)),
            dma((na - 1,)),
            dma((na - 1,)),
            dma((na - 1,)),
            dma((na - 1,)),
            dma((NB - 1,)),
            dma((NB - 1,)),
            dma((NB - 1,)),
            dma((NB - 1,)),
        ],
        compiler_params=pltpu.CompilerParams(
            collective_id=0, has_side_effects=True, vmem_limit_bytes=48 * 1024 * 1024
        ),
    )(lengths, prefill_flag, cache_slot, slot_owner, qkv, cache, out_weight)
    summed = hidden_in.astype(F32) + projected.astype(F32)
    return summed.astype(BF16)


def solution(mesh):
    placed = (
        P("req", None),
        P("req", None),
        P("req", None, None),
        P("req"),
        P("req"),
        P("req"),
        P("req"),
        P(),
    )
    return jax.shard_map(
        functools.partial(local, n=mesh.shape["req"]),
        mesh=mesh,
        in_specs=placed,
        out_specs=P("req", None),
        check_vma=False,
    )
```

```python
import functools
import math

import jax
import jax.numpy as jnp
from jax import lax
from jax.experimental import pallas as pl
from jax.experimental.pallas import tpu as pltpu
from jax.sharding import PartitionSpec as P

D = 2048
H = 16
HD = 128
TOK_DEV = 512
RD = 4
LMAX = 128
NB = 8
HALF = TOK_DEV // 2
CUTS = ((0, 4), (4, 8), (8, 16))
SEG = 4
TAIL = 128
NT = 1024
EXT = D + HD
MARK = 96
SCALE = 1.0 / math.sqrt(HD)
SCALE2 = SCALE * math.log2(math.e)
F32 = jnp.float32
BF16 = jnp.bfloat16
MESH = pl.DeviceIdType.MESH
NEG = float(jnp.finfo(jnp.float32).min)


def score(x, y):
    return lax.dot_general(x, y, (((1,), (1,)), ((), ())), preferred_element_type=F32)


def attend_head(h, qkv, att):
    col = pl.multiple_of(h * HD, HD)
    q = qkv[0, :, pl.ds(col, HD)]
    keys = qkv[1, :, pl.ds(col, HD)]
    ones = jnp.ones((TOK_DEV, HD), BF16)
    values = jnp.concatenate([qkv[2, :, pl.ds(col, HD)], ones], axis=1)
    row = lax.broadcasted_iota(jnp.int32, (HALF, HALF), 0)
    lane = lax.broadcasted_iota(jnp.int32, (HALF, HALF), 1)
    causal = lane <= row
    s_first = score(q, keys[:HALF])
    s_last = jnp.where(causal, score(q[HALF:], keys[HALF:]), NEG)
    s_upper = jnp.where(causal, s_first[:HALF], NEG)
    s_lower = s_first[HALF:]
    top_upper = jnp.max(s_upper, axis=1, keepdims=True)
    top_lower = jnp.max(jnp.maximum(s_lower, s_last), axis=1, keepdims=True)
    p_upper = jnp.exp2((s_upper - top_upper) * SCALE2).astype(BF16)
    p_lower = jnp.exp2((s_lower - top_lower) * SCALE2).astype(BF16)
    p_last = jnp.exp2((s_last - top_lower) * SCALE2).astype(BF16)
    lower = jnp.dot(
        jnp.concatenate([p_lower, p_last], axis=1), values, preferred_element_type=F32
    )
    upper = jnp.dot(p_upper, values[:HALF], preferred_element_type=F32)
    att[pl.ds(0, HALF), pl.ds(col, HD)] = (upper[:, :HD] / upper[:, HD:]).astype(BF16)
    att[pl.ds(HALF, HALF), pl.ds(col, HD)] = (lower[:, :HD] / lower[:, HD:]).astype(BF16)


def head_mask():
    row = lax.broadcasted_iota(jnp.int32, (H, D), 0)
    lane = lax.broadcasted_iota(jnp.int32, (H, D), 1)
    return (lane // HD) == row


def pick_row(block, j):
    row = lax.broadcasted_iota(jnp.int32, block.shape, 0)
    return jnp.sum(jnp.where(row == j, block.astype(F32), 0.0), axis=0, keepdims=True)


def pick_marked(block, place):
    block = block.astype(F32)
    lane = lax.broadcasted_iota(jnp.int32, (2, HD), 1)
    mark = jnp.sum(jnp.where(lane == MARK, block[:, D:], 0.0), axis=1, keepdims=True)
    wanted = mark == place.astype(F32)
    return jnp.sum(jnp.where(wanted, block, 0.0), axis=0, keepdims=True)


def split3(x):
    pieces = []
    for _ in range(3):
        piece = x.astype(BF16).astype(F32)
        pieces.append(piece)
        x = x - piece
    return pieces


def first_two(far):
    one = jnp.int32(-1)
    two = jnp.int32(-1)
    for j in reversed(range(RD)):
        two = jnp.where(far[j], one, two)
        one = jnp.where(far[j], jnp.int32(j), one)
    return one, two


def message(rows, places):
    lane = lax.broadcasted_iota(jnp.int32, (1, EXT), 1)
    row = lax.broadcasted_iota(jnp.int32, (2, EXT), 0)
    marked = [
        jnp.where(lane == D + MARK, place.astype(F32), x) for x, place in zip(rows, places)
    ]
    return jnp.where(row == 0, marked[0], marked[1]).astype(BF16)


def partial(q, slot, cache, lengths, own):
    valid = lax.broadcasted_iota(jnp.int32, (H, LMAX), 1) < lengths[slot]
    q_heads = jnp.where(own, q, 0.0).astype(BF16)
    scores = jnp.where(valid, score(q_heads, cache[slot, :, pl.ds(0, D)]), NEG)
    top = jnp.max(scores, axis=1, keepdims=True)
    p = jnp.where(valid, jnp.exp2((scores - top) * SCALE2), 0.0)
    total = jnp.sum(p, axis=1, keepdims=True)
    o = jnp.dot(p.astype(BF16), cache[slot, :, pl.ds(D, D)], preferred_element_type=F32)
    o = jnp.sum(jnp.where(own, o / total, 0.0), axis=0, keepdims=True)
    row = lax.broadcasted_iota(jnp.int32, (H, HD), 0)
    lane = lax.broadcasted_iota(jnp.int32, (H, HD), 1)
    stats = jnp.zeros((H, HD), F32)
    for k, piece in enumerate(split3(top * SCALE) + split3(total)):
        stats = jnp.where(lane == row + k * H, piece, stats)
    return jnp.concatenate([o, jnp.sum(stats, axis=0, keepdims=True)], axis=1)


def kernel(
    na,
    lengths_hbm,
    flag_hbm,
    cache_slot_hbm,
    slot_owner_hbm,
    hidden_hbm,
    qkv_hbm,
    cache_hbm,
    weight_hbm,
    out_any,
    lengths,
    flag,
    cache_slot,
    slot_owner,
    first,
    hidden,
    qkv,
    cache,
    weight,
    att,
    out,
    local_part,
    qg,
    cg,
    in_sem,
    out_sem,
    sa,
    ra,
    sb,
    rb,
    sc,
    rc,
    sd,
    rd,
):
    me = lax.axis_index("req")
    a = me // NB
    b = me % NB

    def peer_a(t):
        return lax.rem(a + t, na) * NB + b

    def peer_b(t):
        return a * NB + lax.rem(b + t, NB)

    small = [
        pltpu.make_async_copy(src, dst, in_sem.at[i])
        for i, (src, dst) in enumerate(
            [
                (cache_slot_hbm, cache_slot),
                (qkv_hbm.at[pl.ds(0, 16), :], first),
                (lengths_hbm, lengths),
                (slot_owner_hbm, slot_owner),
                (flag_hbm, flag),
            ]
        )
    ]
    load_cache = pltpu.make_async_copy(cache_hbm, cache, in_sem.at[5])
    load_weight = pltpu.make_async_copy(weight_hbm, weight, in_sem.at[6])
    load_hidden = pltpu.make_async_copy(hidden_hbm, hidden, in_sem.at[7])
    loads = []
    for start, stop in CUTS:
        for part in range(3):
            loads.append(
                pltpu.make_async_copy(
                    qkv_hbm.at[:, pl.ds(part * D + start * HD, (stop - start) * HD)],
                    qkv.at[part, :, pl.ds(start * HD, (stop - start) * HD)],
                    in_sem.at[8 + len(loads)],
                )
            )
    for load in small:
        load.start()

    barrier = pltpu.get_barrier_semaphore()

    @pl.loop(1, na)
    def _(t):
        pl.semaphore_signal(barrier, inc=1, device_id=(peer_a(t),), device_id_type=MESH)

    @pl.loop(1, NB)
    def _(t):
        pl.semaphore_signal(barrier, inc=1, device_id=(peer_b(t),), device_id_type=MESH)

    load_cache.start()
    for load in loads:
        load.start()
    load_weight.start()
    load_hidden.start()

    def copy_a(buf, send, recv, t):
        return pltpu.make_async_remote_copy(
            src_ref=buf.at[b, a],
            dst_ref=buf.at[b, a],
            send_sem=send.at[t - 1],
            recv_sem=recv.at[t - 1],
            device_id=(peer_a(t),),
            device_id_type=MESH,
        )

    def copy_b(buf, send, recv, t):
        return pltpu.make_async_remote_copy(
            src_ref=buf.at[b],
            dst_ref=buf.at[b],
            send_sem=send.at[t - 1],
            recv_sem=recv.at[t - 1],
            device_id=(peer_b(t),),
            device_id_type=MESH,
        )

    def start_a(buf, send, recv):
        @pl.loop(1, na)
        def _(t):
            copy_a(buf, send, recv, t).start()

    def wait_a(buf, send, recv):
        @pl.loop(1, na)
        def _(t):
            copy_a(buf, send, recv, t).wait()

    def start_b(buf, send, recv):
        @pl.loop(1, NB)
        def _(t):
            copy_b(buf, send, recv, t).start()

    def wait_b(buf, send, recv):
        @pl.loop(1, NB)
        def _(t):
            copy_b(buf, send, recv, t).wait()

    def segment(g):
        for load in loads[3 * g : 3 * g + 3]:
            load.wait()
        start, stop = CUTS[g]

        @pl.loop(start // SEG, stop // SEG)
        def _(i):
            for u in range(SEG):
                attend_head(i * SEG + u, qkv, att)

    for load in small:
        load.wait()
    own = head_mask()
    mine = first[...].astype(F32)[:8]
    places = first_two([cache_slot[j] // RD != me for j in range(RD)])
    no_stats = jnp.zeros((1, HD), F32)
    qg[b, a] = message(
        [jnp.concatenate([pick_row(mine[:, :D], j), no_stats], axis=1) for j in places], places
    )
    pl.semaphore_wait(barrier, na - 1 + NB - 1)
    start_a(qg, sa, ra)

    load_cache.wait()
    row8 = lax.broadcasted_iota(jnp.int32, (8, EXT), 0)
    held = jnp.zeros((8, EXT), F32)
    for j in range(RD):
        part = partial(mine[j : j + 1, :D], cache_slot[j] % RD, cache, lengths, own)
        held = jnp.where(row8 == j, part, held)
    local_part[...] = held

    wait_a(qg, sa, ra)
    start_b(qg, sb, rb)
    segment(0)
    wait_b(qg, sb, rb)

    places = first_two([slot_owner[s] // RD != me for s in range(RD)])
    rows = []
    for place in places:
        slot = jnp.maximum(place, 0)
        owner = slot_owner[slot]
        device = owner // RD
        q = pick_marked(qg[device % NB, device // NB], owner % RD)
        rows.append(partial(q[:, :D], slot, cache, lengths, own))
    cg[b, a] = message(rows, places)

    start_a(cg, sc, rc)
    segment(1)
    wait_a(cg, sc, rc)
    start_b(cg, sd, rd)
    segment(2)
    load_weight.wait()
    load_hidden.wait()
    is_prefill = flag[0] == 1

    def project(start, stop):
        @pl.loop(0, D // NT)
        def _(n):
            cols = pl.ds(pl.multiple_of(n * NT, NT), NT)
            rows = pl.ds(start, stop - start)
            acc = jnp.dot(att[rows, :], weight[:, cols], preferred_element_type=F32)
            if start >= H:
                acc = jnp.where(is_prefill, acc, 0.0)
            projected = acc.astype(BF16).astype(F32)
            out[rows, cols] = (hidden[rows, cols].astype(F32) + projected).astype(BF16)

        rows = pl.ds(start, stop - start)
        store = pltpu.make_async_copy(
            out.at[rows, :], out_any.at[rows, :], out_sem.at[int(start == 0)]
        )
        store.start()
        return store

    store_lower = project(TAIL, TOK_DEV)
    wait_b(cg, sd, rd)

    row16 = lax.broadcasted_iota(jnp.int32, (H, D), 0)
    row_h = lax.broadcasted_iota(jnp.int32, (H, HD), 0)
    lane_h = lax.broadcasted_iota(jnp.int32, (H, HD), 1)
    diagonal = lane_h % H == row_h
    is_max = jnp.logical_and(diagonal, lane_h < 3 * H)
    is_total = jnp.logical_and(
        diagonal, jnp.logical_and(lane_h >= 3 * H, lane_h < 6 * H)
    )
    decoded = jnp.zeros((H, D), F32)
    for j in range(RD):
        slot = cache_slot[j]
        device = slot // RD
        far = pick_marked(cg[device % NB, device // NB], slot % RD)
        part = jnp.where(device == me, local_part[j : j + 1, :], far)
        co = part[:, :D]
        cm = jnp.sum(jnp.where(is_max, part[:, D:], 0.0), axis=1, keepdims=True)
        cl = jnp.sum(jnp.where(is_total, part[:, D:], 0.0), axis=1, keepdims=True)
        row = mine[j : j + 1]
        product = row[:, :D] * row[:, D : 2 * D]
        ns = jnp.sum(jnp.where(own, product, 0.0), axis=1, keepdims=True) * SCALE
        joint = jnp.maximum(cm, ns)
        wc = cl * jnp.exp(cm - joint)
        wo = jnp.exp(ns - joint)
        mixed = co * (wc / (wc + wo)) + row[:, 2 * D :] * (wo / (wc + wo))
        decoded = jnp.where(
            row16 == j, jnp.sum(jnp.where(own, mixed, 0.0), axis=0, keepdims=True), decoded
        )
    kept = jnp.where(is_prefill, att[pl.ds(0, H), :].astype(F32), decoded)
    att[pl.ds(0, H), :] = kept.astype(BF16)
    rest = att[pl.ds(H, TAIL - H), :]
    att[pl.ds(H, TAIL - H), :] = jnp.where(is_prefill, rest, jnp.zeros_like(rest))
    store_upper = project(0, TAIL)
    store_lower.wait()
    store_upper.wait()


def local(hidden_in, qkv, cache, lengths, prefill_flag, cache_slot, slot_owner, out_weight, n):
    na = n // NB
    hbm = pl.BlockSpec(memory_space=pltpu.HBM)
    dma = pltpu.SemaphoreType.DMA
    return pl.pallas_call(
        functools.partial(kernel, na),
        out_shape=jax.ShapeDtypeStruct((TOK_DEV, D), BF16),
        in_specs=[hbm] * 8,
        out_specs=pl.BlockSpec(memory_space=pl.ANY),
        scratch_shapes=[
            pltpu.SMEM((RD,), jnp.int32),
            pltpu.SMEM((1,), jnp.int32),
            pltpu.SMEM((RD,), jnp.int32),
            pltpu.SMEM((RD,), jnp.int32),
            pltpu.VMEM((16, 3 * D), BF16),
            pltpu.VMEM((TOK_DEV, D), BF16),
            pltpu.VMEM((3, TOK_DEV, D), BF16),
            pltpu.VMEM((RD, LMAX, 2 * D), BF16),
            pltpu.VMEM((D, D), BF16),
            pltpu.VMEM((TOK_DEV, D), BF16),
            pltpu.VMEM((TOK_DEV, D), BF16),
            pltpu.VMEM((8, EXT), F32),
            pltpu.VMEM((NB, na, 2, EXT), BF16),
            pltpu.VMEM((NB, na, 2, EXT), BF16),
            dma((8 + 3 * len(CUTS),)),
            dma((2,)),
            dma((na - 1,)),
            dma((na - 1,)),
            dma((NB - 1,)),
            dma((NB - 1,)),
            dma((na - 1,)),
            dma((na - 1,)),
            dma((NB - 1,)),
            dma((NB - 1,)),
        ],
        compiler_params=pltpu.CompilerParams(
            collective_id=0, has_side_effects=True, vmem_limit_bytes=61 * 1024 * 1024
        ),
    )(
        lengths,
        prefill_flag,
        cache_slot,
        slot_owner,
        hidden_in,
        qkv,
        cache,
        out_weight,
    )


def solution(mesh):
    placed = (
        P("req", None),
        P("req", None),
        P("req", None, None),
        P("req"),
        P("req"),
        P("req"),
        P("req"),
        P(),
    )
    return jax.shard_map(
        functools.partial(local, n=mesh.shape["req"]),
        mesh=mesh,
        in_specs=placed,
        out_specs=P("req", None),
        check_vma=False,
    )
```

```python
import functools
import math

import jax
import jax.numpy as jnp
from jax import lax
from jax.experimental import pallas as pl
from jax.experimental.pallas import tpu as pltpu
from jax.sharding import PartitionSpec as P

D = 2048
H = 16
HD = 128
TOK_DEV = 512
RD = 4
LMAX = 128
NB = 8
HALF = TOK_DEV // 2
CUTS = ((0, 6), (6, 12), (12, 16))
TAIL = 128
NT = 1024
EXT = D + HD
MARK = 96
SCALE = 1.0 / math.sqrt(HD)
SCALE2 = SCALE * math.log2(math.e)
F32 = jnp.float32
BF16 = jnp.bfloat16
MESH = pl.DeviceIdType.MESH
NEG = float(jnp.finfo(jnp.float32).min)


def score(x, y):
    return lax.dot_general(x, y, (((1,), (1,)), ((), ())), preferred_element_type=F32)


def attend_head(h, qkv, att):
    col = h * HD
    q = qkv[0, :, pl.ds(col, HD)]
    keys = qkv[1, :, pl.ds(col, HD)]
    ones = jnp.ones((TOK_DEV, HD), BF16)
    values = jnp.concatenate([qkv[2, :, pl.ds(col, HD)], ones], axis=1)
    row = lax.broadcasted_iota(jnp.int32, (HALF, HALF), 0)
    lane = lax.broadcasted_iota(jnp.int32, (HALF, HALF), 1)
    causal = lane <= row
    s_first = score(q, keys[:HALF])
    s_last = jnp.where(causal, score(q[HALF:], keys[HALF:]), NEG)
    s_upper = jnp.where(causal, s_first[:HALF], NEG)
    s_lower = s_first[HALF:]
    top_upper = jnp.max(s_upper, axis=1, keepdims=True)
    top_lower = jnp.max(jnp.maximum(s_lower, s_last), axis=1, keepdims=True)
    p_upper = jnp.exp2((s_upper - top_upper) * SCALE2).astype(BF16)
    p_lower = jnp.exp2((s_lower - top_lower) * SCALE2).astype(BF16)
    p_last = jnp.exp2((s_last - top_lower) * SCALE2).astype(BF16)
    lower = jnp.dot(
        jnp.concatenate([p_lower, p_last], axis=1), values, preferred_element_type=F32
    )
    upper = jnp.dot(p_upper, values[:HALF], preferred_element_type=F32)
    att[pl.ds(0, HALF), pl.ds(col, HD)] = (upper[:, :HD] / upper[:, HD:]).astype(BF16)
    att[pl.ds(HALF, HALF), pl.ds(col, HD)] = (lower[:, :HD] / lower[:, HD:]).astype(BF16)


def head_mask():
    row = lax.broadcasted_iota(jnp.int32, (H, D), 0)
    lane = lax.broadcasted_iota(jnp.int32, (H, D), 1)
    return (lane // HD) == row


def pick_row(block, j):
    row = lax.broadcasted_iota(jnp.int32, block.shape, 0)
    return jnp.sum(jnp.where(row == j, block.astype(F32), 0.0), axis=0, keepdims=True)


def pick_marked(block, place):
    block = block.astype(F32)
    lane = lax.broadcasted_iota(jnp.int32, (2, HD), 1)
    mark = jnp.sum(jnp.where(lane == MARK, block[:, D:], 0.0), axis=1, keepdims=True)
    wanted = mark == place.astype(F32)
    return jnp.sum(jnp.where(wanted, block, 0.0), axis=0, keepdims=True)


def split3(x):
    pieces = []
    for _ in range(3):
        piece = x.astype(BF16).astype(F32)
        pieces.append(piece)
        x = x - piece
    return pieces


def first_two(far):
    one = jnp.int32(-1)
    two = jnp.int32(-1)
    for j in reversed(range(RD)):
        two = jnp.where(far[j], one, two)
        one = jnp.where(far[j], jnp.int32(j), one)
    return one, two


def message(rows, places):
    lane = lax.broadcasted_iota(jnp.int32, (1, EXT), 1)
    row = lax.broadcasted_iota(jnp.int32, (2, EXT), 0)
    marked = [
        jnp.where(lane == D + MARK, place.astype(F32), x) for x, place in zip(rows, places)
    ]
    return jnp.where(row == 0, marked[0], marked[1]).astype(BF16)


def partial(q, slot, cache, table, own):
    valid = lax.broadcasted_iota(jnp.int32, (H, LMAX), 1) < table[slot]
    q_heads = jnp.where(own, q, 0.0).astype(BF16)
    scores = jnp.where(valid, score(q_heads, cache[slot, :, pl.ds(0, D)]), NEG)
    top = jnp.max(scores, axis=1, keepdims=True)
    p = jnp.where(valid, jnp.exp2((scores - top) * SCALE2), 0.0)
    total = jnp.sum(p, axis=1, keepdims=True)
    o = jnp.dot(p.astype(BF16), cache[slot, :, pl.ds(D, D)], preferred_element_type=F32)
    o = jnp.sum(jnp.where(own, o / total, 0.0), axis=0, keepdims=True)
    row = lax.broadcasted_iota(jnp.int32, (H, HD), 0)
    lane = lax.broadcasted_iota(jnp.int32, (H, HD), 1)
    stats = jnp.zeros((H, HD), F32)
    for k, piece in enumerate(split3(top * SCALE) + split3(total)):
        stats = jnp.where(lane == row + k * H, piece, stats)
    return jnp.concatenate([o, jnp.sum(stats, axis=0, keepdims=True)], axis=1)


def kernel(
    na,
    table_hbm,
    qkv_hbm,
    cache_hbm,
    weight_hbm,
    out_any,
    table,
    first,
    qkv,
    cache,
    weight,
    att,
    out,
    local_part,
    qg,
    cg,
    in_sem,
    out_sem,
    sa,
    ra,
    sb,
    rb,
    sc,
    rc,
    sd,
    rd,
):
    me = lax.axis_index("req")
    a = me // NB
    b = me % NB

    def peer_a(t):
        return lax.rem(a + t, na) * NB + b

    def peer_b(t):
        return a * NB + lax.rem(b + t, NB)

    small = [
        pltpu.make_async_copy(src, dst, in_sem.at[i])
        for i, (src, dst) in enumerate(
            [
                (table_hbm, table),
                (qkv_hbm.at[pl.ds(0, 16), :], first),
            ]
        )
    ]
    load_cache = pltpu.make_async_copy(cache_hbm, cache, in_sem.at[5])
    load_weight = pltpu.make_async_copy(weight_hbm, weight, in_sem.at[6])
    loads = []
    for start, stop in CUTS:
        for part in range(3):
            loads.append(
                pltpu.make_async_copy(
                    qkv_hbm.at[:, pl.ds(part * D + start * HD, (stop - start) * HD)],
                    qkv.at[part, :, pl.ds(start * HD, (stop - start) * HD)],
                    in_sem.at[8 + len(loads)],
                )
            )
    for load in small:
        load.start()

    barrier = pltpu.get_barrier_semaphore()

    @pl.loop(1, na)
    def _(t):
        pl.semaphore_signal(barrier, inc=1, device_id=(peer_a(t),), device_id_type=MESH)

    @pl.loop(1, NB)
    def _(t):
        pl.semaphore_signal(barrier, inc=1, device_id=(peer_b(t),), device_id_type=MESH)

    load_cache.start()
    for load in loads:
        load.start()
    load_weight.start()

    def copy_a(buf, send, recv, t):
        return pltpu.make_async_remote_copy(
            src_ref=buf.at[b, a],
            dst_ref=buf.at[b, a],
            send_sem=send.at[t - 1],
            recv_sem=recv.at[t - 1],
            device_id=(peer_a(t),),
            device_id_type=MESH,
        )

    def copy_b(buf, send, recv, t):
        return pltpu.make_async_remote_copy(
            src_ref=buf.at[b],
            dst_ref=buf.at[b],
            send_sem=send.at[t - 1],
            recv_sem=recv.at[t - 1],
            device_id=(peer_b(t),),
            device_id_type=MESH,
        )

    def start_a(buf, send, recv):
        @pl.loop(1, na)
        def _(t):
            copy_a(buf, send, recv, t).start()

    def wait_a(buf, send, recv):
        @pl.loop(1, na)
        def _(t):
            copy_a(buf, send, recv, t).wait()

    def start_b(buf, send, recv):
        @pl.loop(1, NB)
        def _(t):
            copy_b(buf, send, recv, t).start()

    def wait_b(buf, send, recv):
        @pl.loop(1, NB)
        def _(t):
            copy_b(buf, send, recv, t).wait()

    def segment(g):
        for load in loads[3 * g : 3 * g + 3]:
            load.wait()
        start, stop = CUTS[g]

        for h in range(start, stop):
            attend_head(h, qkv, att)

    for load in small:
        load.wait()
    own = head_mask()
    mine = first[...].astype(F32)[:8]
    places = first_two([table[RD + j] // RD != me for j in range(RD)])
    no_stats = jnp.zeros((1, HD), F32)
    qg[b, a] = message(
        [jnp.concatenate([pick_row(mine[:, :D], j), no_stats], axis=1) for j in places], places
    )
    pl.semaphore_wait(barrier, na - 1 + NB - 1)
    start_a(qg, sa, ra)

    load_cache.wait()
    row8 = lax.broadcasted_iota(jnp.int32, (8, EXT), 0)
    held = jnp.zeros((8, EXT), F32)
    for j in range(RD):
        part = partial(mine[j : j + 1, :D], table[RD + j] % RD, cache, table, own)
        held = jnp.where(row8 == j, part, held)
    local_part[...] = held

    wait_a(qg, sa, ra)
    start_b(qg, sb, rb)
    segment(0)
    wait_b(qg, sb, rb)

    places = first_two([table[2 * RD + s] // RD != me for s in range(RD)])
    rows = []
    for place in places:
        slot = jnp.maximum(place, 0)
        owner = table[2 * RD + slot]
        device = owner // RD
        q = pick_marked(qg[device % NB, device // NB], owner % RD)
        rows.append(partial(q[:, :D], slot, cache, table, own))
    cg[b, a] = message(rows, places)

    start_a(cg, sc, rc)
    segment(1)
    wait_a(cg, sc, rc)
    start_b(cg, sd, rd)
    segment(2)
    load_weight.wait()
    is_prefill = table[3 * RD] == 1

    def project(start, stop):
        @pl.loop(0, D // NT)
        def _(n):
            cols = pl.ds(pl.multiple_of(n * NT, NT), NT)
            rows = pl.ds(start, stop - start)
            acc = jnp.dot(att[rows, :], weight[:, cols], preferred_element_type=F32)
            if start >= H:
                acc = jnp.where(is_prefill, acc, 0.0)
            out[rows, cols] = acc.astype(BF16)

        rows = pl.ds(start, stop - start)
        store = pltpu.make_async_copy(
            out.at[rows, :], out_any.at[rows, :], out_sem.at[int(start == 0)]
        )
        store.start()
        return store

    own_scores = []
    for j in range(RD):
        product = mine[j : j + 1, :D] * mine[j : j + 1, D : 2 * D]
        own_scores.append(
            jnp.sum(jnp.where(own, product, 0.0), axis=1, keepdims=True) * SCALE
        )

    store_lower = project(TAIL, TOK_DEV)
    wait_b(cg, sd, rd)

    row16 = lax.broadcasted_iota(jnp.int32, (H, D), 0)
    row_h = lax.broadcasted_iota(jnp.int32, (H, HD), 0)
    lane_h = lax.broadcasted_iota(jnp.int32, (H, HD), 1)
    diagonal = lane_h % H == row_h
    is_max = jnp.logical_and(diagonal, lane_h < 3 * H)
    is_total = jnp.logical_and(
        diagonal, jnp.logical_and(lane_h >= 3 * H, lane_h < 6 * H)
    )
    decoded = jnp.zeros((H, D), F32)
    for j in range(RD):
        slot = table[RD + j]
        device = slot // RD
        far = pick_marked(cg[device % NB, device // NB], slot % RD)
        part = jnp.where(device == me, local_part[j : j + 1, :], far)
        co = part[:, :D]
        cm = jnp.sum(jnp.where(is_max, part[:, D:], 0.0), axis=1, keepdims=True)
        cl = jnp.sum(jnp.where(is_total, part[:, D:], 0.0), axis=1, keepdims=True)
        row = mine[j : j + 1]
        ns = own_scores[j]
        joint = jnp.maximum(cm, ns)
        wc = cl * jnp.exp(cm - joint)
        wo = jnp.exp(ns - joint)
        mixed = co * (wc / (wc + wo)) + row[:, 2 * D :] * (wo / (wc + wo))
        decoded = jnp.where(
            row16 == j, jnp.sum(jnp.where(own, mixed, 0.0), axis=0, keepdims=True), decoded
        )
    kept = jnp.where(is_prefill, att[pl.ds(0, H), :].astype(F32), decoded)
    att[pl.ds(0, H), :] = kept.astype(BF16)
    rest = att[pl.ds(H, TAIL - H), :]
    att[pl.ds(H, TAIL - H), :] = jnp.where(is_prefill, rest, jnp.zeros_like(rest))
    store_upper = project(0, TAIL)
    store_lower.wait()
    store_upper.wait()


def local(hidden_in, qkv, cache, lengths, prefill_flag, cache_slot, slot_owner, out_weight, n):
    na = n // NB
    hbm = pl.BlockSpec(memory_space=pltpu.HBM)
    dma = pltpu.SemaphoreType.DMA
    table = jnp.concatenate([lengths, cache_slot, slot_owner, prefill_flag])
    projected = pl.pallas_call(
        functools.partial(kernel, na),
        out_shape=jax.ShapeDtypeStruct((TOK_DEV, D), BF16),
        in_specs=[hbm] * 4,
        out_specs=pl.BlockSpec(memory_space=pl.ANY),
        scratch_shapes=[
            pltpu.SMEM((3 * RD + 1,), jnp.int32),
            pltpu.VMEM((16, 3 * D), BF16),
            pltpu.VMEM((3, TOK_DEV, D), BF16),
            pltpu.VMEM((RD, LMAX, 2 * D), BF16),
            pltpu.VMEM((D, D), BF16),
            pltpu.VMEM((TOK_DEV, D), BF16),
            pltpu.VMEM((TOK_DEV, D), BF16),
            pltpu.VMEM((8, EXT), F32),
            pltpu.VMEM((NB, na, 2, EXT), BF16),
            pltpu.VMEM((NB, na, 2, EXT), BF16),
            dma((8 + 3 * len(CUTS),)),
            dma((2,)),
            dma((na - 1,)),
            dma((na - 1,)),
            dma((NB - 1,)),
            dma((NB - 1,)),
            dma((na - 1,)),
            dma((na - 1,)),
            dma((NB - 1,)),
            dma((NB - 1,)),
        ],
        compiler_params=pltpu.CompilerParams(
            collective_id=0, has_side_effects=True, vmem_limit_bytes=48 * 1024 * 1024
        ),
    )(
        table,
        qkv,
        cache,
        out_weight,
    )
    return (hidden_in.astype(F32) + projected.astype(F32)).astype(BF16)


def solution(mesh):
    placed = (
        P("req", None),
        P("req", None),
        P("req", None, None),
        P("req"),
        P("req"),
        P("req"),
        P("req"),
        P(),
    )
    return jax.shard_map(
        functools.partial(local, n=mesh.shape["req"]),
        mesh=mesh,
        in_specs=placed,
        out_specs=P("req", None),
        check_vma=False,
    )
```
